256 devices in a mesh: ex: 32 (over x, z), feat: 8 (over y, core).
Axes of the slice: x: 4, y: 4, z: 8, core: 2. Of those that a mesh axis runs over, the one named last changes fastest.
Arguments:
- train_grads: bfloat16 [16384, 32768], P('ex', 'feat'), may hold values from -0.03125 to 0.03125
- audit_grads: bfloat16 [2, 32, 32, 32768], P(None, 'ex', None, 'feat'), may hold values from -6 to 6
- owner_map: int32 [64], replicated, may hold values from 0 to 63, as said below
- pair_blocks: int32 [32, 32], P('ex'), may hold values from 0 to 63, as said below
- pair_counts: int32 [32], P('ex'), may hold values from 1 to 32, as said below
Outputs:
- tiles: float32 [32, 32, 32, 512], P('ex', 'feat')
The draws below stay inside these ranges and needn't reach their ends.
Inputs may be any that keep to these rules, and one draw needn't show every extreme that they name: `owner_map`: a permutation of the audit blocks. `pair_blocks`: the 32 entries of each training block name audit blocks whose stored blocks lie on 32 different indices of ex (owner_map[a] % 32 differs); entries at or after pair_counts are not live. `pair_counts`: some training block has all 32 pairs live.
All inputs are finite; a program needn't handle non-finite values.
Results may differ from the reference program's by a relative error of at most 0.0003.
Values may be sent and summed in bfloat16 or wider, within the bound.
A program may use at most 64 MiB of HBM per device.

```python
import jax
import jax.numpy as jnp
from jax import lax

F = 32768
TB = 512
AB = 32
ABLK_DEV = 2
NTB = 32
NAB = 64


def layout_tables(key):
    storage = jax.random.permutation(jax.random.fold_in(key, 11), NAB).astype(jnp.int32)
    inverse = jnp.argsort(storage).astype(jnp.int32)
    row_keys = jax.random.split(jax.random.fold_in(key, 12), NTB)

    def shuffle_row(row_key):
        return jax.random.permutation(row_key, NTB)
    owners = jax.vmap(shuffle_row)(row_keys).astype(jnp.int32)
    local = jax.random.randint(jax.random.fold_in(key, 13), (NTB, NTB), 0, ABLK_DEV, dtype=jnp.int32)
    pairs = jnp.take(inverse, local * NTB + owners)
    return (storage, pairs.astype(jnp.int32))


def draw_owner_map(key, part):
    storage, pairs = layout_tables(key)
    return storage


def draw_pair_blocks(key, part):
    storage, pairs = layout_tables(key)
    return pairs


def draw_pair_counts(key, part):
    first = jax.random.randint(jax.random.fold_in(key, 21), (NTB,), 1, NTB + 1, dtype=jnp.int32)
    second = jax.random.randint(jax.random.fold_in(key, 22), (NTB,), 1, NTB + 1, dtype=jnp.int32)
    counts = jnp.minimum(first, second)
    hottest = jax.random.randint(jax.random.fold_in(key, 23), (), 0, NTB, dtype=jnp.int32)
    return jnp.where(jnp.arange(NTB, dtype=jnp.int32) == hottest, NTB, counts).astype(jnp.int32)


def level_of(key, dims, shards, least, top_value):
    def one(position, shards_of):
        steps = jax.random.uniform(jax.random.fold_in(jax.random.fold_in(key, 6), position), (shards_of,), jnp.float32, least / len(shards), top_value / len(shards))
        return jnp.repeat(jnp.exp(steps), dims[position] // shards_of).reshape((-1,) + (1,) * (len(dims) - position - 1))

    level = one(*shards[0])
    for cut in shards[1:]:
        level = level * one(*cut)
    return level


def normal_values(key, extent, width, reach, cuts=(), kind=jnp.bfloat16):
    gain = level_of(key, extent, cuts, -0.22, 0.18) if cuts else 1.0
    result = jax.random.normal(key, extent, jnp.float32) * width * gain
    return jnp.minimum(jnp.maximum(result, -reach), reach).astype(kind)


def setup_inputs(seed: int = 0) -> dict:
    keys = jax.random.split(jax.random.key(seed), 6)
    return {
        "train_grads": normal_values(keys[0], (NTB * TB, F), F ** -0.5, 0.03125, ((0, 32), (1, 8))),
        "audit_grads": normal_values(keys[1], (ABLK_DEV, NTB, AB, F), 1.0, 6.0, ((1, 32), (3, 8))),
        "owner_map": draw_owner_map(jax.random.fold_in(keys[5], 71), 0),
        "pair_blocks": draw_pair_blocks(jax.random.fold_in(keys[5], 71), 0),
        "pair_counts": draw_pair_counts(jax.random.fold_in(keys[5], 71), 0),
    }


def reference(train_grads, audit_grads, owner_map, pair_blocks, pair_counts):
    blocks = train_grads.reshape(NTB, TB, F)
    order = jnp.arange(NTB, dtype=jnp.int32)

    def score_block(index):
        stored = jnp.take(owner_map, pair_blocks[index])
        rows = audit_grads[stored // NTB, stored % NTB]
        flat = rows.reshape(NTB * AB, F)
        scores = jnp.dot(flat, blocks[index].T, preferred_element_type=jnp.float32).reshape(NTB, AB, TB)
        live = (order < pair_counts[index]).astype(jnp.float32)
        return scores * live[:, None, None]

    return lax.map(score_block, jnp.arange(NTB, dtype=jnp.int32))
```

```python
import functools

import jax
import jax.numpy as jnp
from jax import lax
from jax.experimental import pallas as pl
from jax.experimental.pallas import tpu as pltpu
from jax.sharding import PartitionSpec as P

MESH = pl.DeviceIdType.MESH
NX, NZ, NY = 4, 8, 4
HOLDERS = NX * NZ
MESSAGES = 96
CHUNK = 1024


def kernel(train_hbm, audit_hbm, owner, pairs, counts, out, *scratch):
    (train, table, tabs, scores, pack, pack_in, ysend, yrecv, send_sem, recv_sem, local_sem) = scratch[:11]
    z_bufs = scratch[11:19]
    o_full = dict(zip((0, 1, 2, 6, 7), scratch[19:24]))
    o_sel, near_up, near_down, stage = scratch[24:28]
    ex, feat = lax.axis_index("ex"), lax.axis_index("feat")
    x, z, y, c = ex // NZ, ex % NZ, feat // 2, feat % 2
    width = train.shape[1]

    def at(dx=0, dz=0, dy=0, dc=0):
        px, pz = (x + dx + NX) % NX, (z + dz + NZ) % NZ
        py, pc = (y + dy + NY) % NY, (c + dc) % 2
        return (px * NZ + pz, py * 2 + pc)

    right, left, across = at(dx=1), at(dx=-1), at(dx=2)
    up, down, partner = at(dz=1), at(dz=-1), at(dc=1)
    ys = [at(dy=d) for d in (1, 2, 3)]

    barrier = pltpu.get_barrier_semaphore()
    everyone = [right, left, across, up, down, partner] + ys
    for peer in everyone:
        pl.semaphore_signal(barrier, inc=1, device_id=peer, device_id_type=MESH)
    own_copy = pltpu.make_async_copy(audit_hbm.at[:, 0], z_bufs[0], local_sem.at[0])
    own_copy.start()
    train_copy = pltpu.make_async_copy(train_hbm, train, local_sem.at[1])
    train_copy.start()

    def stored_of(k):
        return owner[pairs[0, k]]

    lane = lax.broadcasted_iota(jnp.int32, (8, 128), 1)
    picks = jnp.zeros((8, 128), jnp.int32)
    for k in range(HOLDERS):
        stored = stored_of(k)
        picks = jnp.where(lane == lax.rem(stored, HOLDERS), lax.div(stored, HOLDERS), picks)
    table[...] = picks

    def choice(ref, dx, dz):
        holder = (x + dx + NX) % NX * NZ + (z + dz + NZ) % NZ
        return jnp.max(jnp.where(lane == holder, ref[...], 0))

    count = [0]
    sent = []

    def send(src, dst, peer):
        i = count[0]
        count[0] += 1
        copy = pltpu.make_async_remote_copy(
            src_ref=src, dst_ref=dst, send_sem=send_sem.at[i], recv_sem=recv_sem.at[i], device_id=peer, device_id_type=MESH
        )
        copy.start()
        sent.append(copy)
        return copy

    pl.semaphore_wait(barrier, len(everyone))
    own_copy.wait()

    talk = [
        send(table, tabs.at[1], right),
        send(table, tabs.at[0], left),
        send(table, tabs.at[2], across),
        send(table, tabs.at[4], up),
        send(table, tabs.at[3], down),
    ]
    zc = {}
    oc = {}

    def z_forward(d, j, sign):
        to = (d + sign) % NZ
        zc[to, j] = send(z_bufs[d].at[j], z_bufs[to].at[j], up if sign > 0 else down)

    def o_forward(d, sign):
        to = (d + sign) % NZ
        oc[to] = [send(o_full[d].at[j], o_full[to].at[j], up if sign > 0 else down) for j in range(2)]

    for j in range(2):
        z_forward(0, j, 1)
        z_forward(0, j, -1)
    oc[0] = [send(z_bufs[0].at[j], o_full[0].at[j], across) for j in range(2)]

    for copy in talk:
        copy.wait_recv()

    slot = [0]
    nu, nd = {}, {}

    def staged(src, pick):
        i = slot[0]
        slot[0] += 1
        stage[i] = src[pick]
        return stage.at[i]

    def x_forward(d):
        a = staged(z_bufs[d], choice(tabs.at[0], 0, -d))
        b = staged(z_bufs[d], choice(tabs.at[1], 0, -d))
        nd[d] = send(a, near_down.at[d], right)
        nu[d] = send(b, near_up.at[d], left)

    def z_arrive(d, j, sign=None):
        zc[d, j].wait_recv()
        if sign is not None:
            z_forward(d, j, sign)

    def o_arrive(d):
        for copy in oc[d]:
            copy.wait_recv()

    def own(d):
        return d, lambda k: z_bufs[d][choice_of[0, d], :, k]

    def plus(d):
        return NZ + d, lambda k: near_up[d, :, k]

    def minus(d):
        return 3 * NZ + d, lambda k: near_down[d, :, k]

    def far(d):
        if d in o_full:
            return 2 * NZ + d, lambda k: o_full[d][choice_of[2, d], :, k]
        return 2 * NZ + d, lambda k: o_sel[d - 3, :, k]

    choice_of = {}

    def settle(rel, d):
        choice_of[rel, d] = choice(table, rel, -d)

    def multiply(rows):
        for part in range(width // CHUNK):
            k = pl.ds(part * CHUNK, CHUNK)
            lhs = jnp.concatenate([load(k) for _, load in rows], axis=0)
            got = lax.dot_general(lhs, train[:, k], (((1,), (1,)), ((), ())), preferred_element_type=jnp.float32)
            for i, (s, _) in enumerate(rows):
                tile = got[i * 32 : (i + 1) * 32]
                scores[s] = tile if part == 0 else scores[s] + tile

    x_forward(0)
    for d, sign in ((1, 1), (7, -1)):
        z_arrive(d, 0, sign)
    for d, sign in ((1, 1), (7, -1)):
        z_arrive(d, 1, sign)
    x_forward(1)
    x_forward(7)
    for d, sign in ((2, 1), (6, -1)):
        z_arrive(d, 0, sign)
    for d, sign in ((2, 1), (6, -1)):
        z_arrive(d, 1, sign)
    o_arrive(0)
    o_forward(0, 1)
    o_forward(0, -1)
    x_forward(2)
    x_forward(6)
    train_copy.wait()
    for d in (0, 1, 2, 6, 7):
        settle(2, d)
    for d in range(NZ):
        settle(0, d)
    nu[0].wait_recv()
    nd[0].wait_recv()
    multiply([own(0), plus(0), minus(0), far(0)])
    z_arrive(3, 0, 1)
    z_arrive(5, 0)
    z_arrive(3, 1)
    z_arrive(5, 1, -1)
    x_forward(3)
    x_forward(5)
    for d in (1, 7):
        nu[d].wait_recv()
        nd[d].wait_recv()
    multiply([own(1), plus(1), minus(1), own(7), plus(7), minus(7)])
    z_arrive(4, 0)
    z_arrive(4, 1)
    x_forward(4)
    oc[4] = send(staged(z_bufs[4], choice(tabs.at[2], 0, -4)), o_sel.at[1], across)
    for d in (2, 6):
        nu[d].wait_recv()
        nd[d].wait_recv()
    multiply([own(2), plus(2), minus(2), own(6), plus(6), minus(6)])
    o_arrive(1)
    o_forward(1, 1)
    o_arrive(7)
    o_forward(7, -1)
    for d in (3, 5):
        nu[d].wait_recv()
        nd[d].wait_recv()
    multiply([own(3), plus(3), minus(3), own(5), plus(5), minus(5)])
    o_arrive(2)
    oc[3] = send(staged(o_full[2], choice(tabs.at[3], 2, -2)), o_sel.at[0], up)
    o_arrive(6)
    oc[5] = send(staged(o_full[6], choice(tabs.at[4], 2, 2)), o_sel.at[2], down)
    multiply([far(1), far(7), far(2), far(6)])
    nu[4].wait_recv()
    nd[4].wait_recv()
    oc[4].wait_recv()
    multiply([own(4), plus(4), minus(4), far(4)])
    oc[3].wait_recv()
    oc[5].wait_recv()
    multiply([far(3), far(5)])

    def tile(dy, core, i):
        k = 4 * (2 * ((y + dy) % NY) + core) + i
        holder = lax.rem(stored_of(k), HOLDERS)
        rel = lax.rem(lax.div(holder, NZ) - x + NX, NX)
        d = lax.rem(z - lax.rem(holder, NZ) + NZ, NZ)
        return jnp.where(k < counts[0], scores[rel * NZ + d], 0.0)

    swaps = {}
    for dy in (2, 1, 3, 0):
        for i in range(4):
            pack[dy, i] = tile(dy, 1 - c, i)
        swaps[dy] = send(pack.at[dy], pack_in.at[dy], partner)
    moves = {}
    for dy in (2, 1, 3):
        swaps[dy].wait_recv()
        for i in range(4):
            ysend[dy - 1, i] = tile(dy, c, i) + pack_in[dy, i]
        moves[dy] = send(ysend.at[dy - 1], yrecv.at[dy - 1], ys[dy - 1])
    swaps[0].wait_recv()
    for i in range(4):
        out[0, i] = tile(0, c, i) + pack_in[0, i]
    for dy in (1, 3, 2):
        moves[dy].wait_recv()
        for i in range(4):
            out[0, i] += yrecv[dy - 1, i]
    for copy in sent:
        copy.wait_send()


def shards(train_grads, audit_grads, owner_map, pair_blocks, pair_counts):
    rows, width = train_grads.shape
    block = (audit_grads.shape[2], width)
    half = pltpu.VMEM
    scratch = [
        half((rows, width), jnp.bfloat16),
        half((8, 128), jnp.int32),
        half((5, 8, 128), jnp.int32),
        half((HOLDERS, block[0], rows), jnp.float32),
        half((NY, 4, block[0], rows), jnp.float32),
        half((NY, 4, block[0], rows), jnp.float32),
        half((NY - 1, 4, block[0], rows), jnp.float32),
        half((NY - 1, 4, block[0], rows), jnp.float32),
        pltpu.SemaphoreType.DMA((MESSAGES,)),
        pltpu.SemaphoreType.DMA((MESSAGES,)),
        pltpu.SemaphoreType.DMA((2,)),
    ]
    scratch += [half((2,) + block, jnp.bfloat16) for _ in range(NZ + 5)]
    scratch += [
        half((3,) + block, jnp.bfloat16),
        half((NZ,) + block, jnp.bfloat16),
        half((NZ,) + block, jnp.bfloat16),
        half((19,) + block, jnp.bfloat16),
    ]
    return pl.pallas_call(
        kernel,
        out_shape=jax.ShapeDtypeStruct((1, 4, block[0], rows), jnp.float32),
        in_specs=[pl.BlockSpec(memory_space=pl.ANY)] * 2 + [pl.BlockSpec(memory_space=pltpu.SMEM)] * 3,
        out_specs=pl.BlockSpec(memory_space=pltpu.VMEM),
        scratch_shapes=scratch,
        compiler_params=pltpu.CompilerParams(collective_id=0, has_side_effects=True, vmem_limit_bytes=60000 * 1024),
    )(train_grads, audit_grads, owner_map, pair_blocks, pair_counts)


def solution(mesh):
    in_specs = (P("ex", "feat"), P(None, "ex", None, "feat"), P(), P("ex", None), P("ex"))
    out_specs = P("ex", "feat", None, None)
    return jax.shard_map(shards, mesh=mesh, in_specs=in_specs, out_specs=out_specs, check_vma=False)
```

```python
import functools

import jax
import jax.numpy as jnp
from jax import lax
from jax.experimental import pallas as pl
from jax.experimental.pallas import tpu as pltpu
from jax.sharding import PartitionSpec as P

MESH = pl.DeviceIdType.MESH
NX, NZ, NY = 4, 8, 4
HOLDERS = NX * NZ
MESSAGES = 160
HALF, LANES = 16, 128
GROUPS = (
    ((0, 0), (1, 0), (3, 0), (2, 0)),
    ((0, 1), (1, 1), (3, 1), (0, 7), (1, 7), (3, 7)),
    ((0, 2), (1, 2), (3, 2), (0, 6), (1, 6), (3, 6)),
    ((0, 3), (1, 3), (3, 3), (0, 5), (1, 5), (3, 5)),
    ((2, 1), (2, 7)),
    ((0, 4), (1, 4), (3, 4)),
    ((2, 2), (2, 6), (2, 4)),
    ((2, 3), (2, 5)),
)
ORDER = [tile for group in GROUPS for tile in group]
SPLIT = (0, 1408, 2688, 4096)
CHUNK = 1024


def kernel(train_hbm, audit_hbm, owner, pairs, counts, out, *scratch):
    (train, table, tabs, scores, other, both, parts, lates, final, place, send_sem, recv_sem, local_sem) = scratch[:13]
    z_bufs = scratch[13:21]
    o_full = dict(zip((0, 1, 2, 6, 7), scratch[21:26]))
    o_sel, near_up, near_down, stage = scratch[26:30]
    ex, feat = lax.axis_index("ex"), lax.axis_index("feat")
    x, z, y, c = ex // NZ, ex % NZ, feat // 2, feat % 2
    width = train.shape[1]

    def at(dx=0, dz=0, dy=0, dc=0):
        px, pz = (x + dx + NX) % NX, (z + dz + NZ) % NZ
        py, pc = (y + dy + NY) % NY, (c + dc) % 2
        return (px * NZ + pz, py * 2 + pc)

    right, left, across = at(dx=1), at(dx=-1), at(dx=2)
    up, down, partner = at(dz=1), at(dz=-1), at(dc=1)
    ys = {(dy, dc): at(dy=dy, dc=dc) for dy in (1, 2, 3) for dc in (0, 1)}
    ys[0, 1] = partner

    barrier = pltpu.get_barrier_semaphore()
    everyone = [right, left, across, up, down] + list(ys.values())
    for peer in everyone:
        pl.semaphore_signal(barrier, inc=1, device_id=peer, device_id_type=MESH)
    own_copy = pltpu.make_async_copy(audit_hbm.at[:, 0], z_bufs[0], local_sem.at[0])
    own_copy.start()
    train_copy = pltpu.make_async_copy(train_hbm, train, local_sem.at[1])
    train_copy.start()

    def stored_of(k):
        return owner[pairs[0, k]]

    lane = lax.broadcasted_iota(jnp.int32, (8, 128), 1)
    picks = jnp.zeros((8, 128), jnp.int32)
    for k in range(HOLDERS):
        stored = stored_of(k)
        picks = jnp.where(lane == lax.rem(stored, HOLDERS), lax.div(stored, HOLDERS), picks)
    table[...] = picks
    for i, (rel, d) in enumerate(ORDER):
        place[rel * NZ + d] = i

    def choice(ref, dx, dz):
        holder = (x + dx + NX) % NX * NZ + (z + dz + NZ) % NZ
        return jnp.max(jnp.where(lane == holder, ref[...], 0))

    count = [0]
    sent = []

    def send(src, dst, peer):
        i = count[0]
        count[0] += 1
        copy = pltpu.make_async_remote_copy(
            src_ref=src, dst_ref=dst, send_sem=send_sem.at[i], recv_sem=recv_sem.at[i], device_id=peer, device_id_type=MESH
        )
        copy.start()
        sent.append(copy)
        return copy

    pl.semaphore_wait(barrier, len(everyone))
    own_copy.wait()

    talk = [
        send(table, tabs.at[1], right),
        send(table, tabs.at[0], left),
        send(table, tabs.at[2], across),
        send(table, tabs.at[4], up),
        send(table, tabs.at[3], down),
    ]
    zc = {}
    oc = {}

    def z_forward(d, j, sign):
        to = (d + sign) % NZ
        zc[to, j] = send(z_bufs[d].at[j], z_bufs[to].at[j], up if sign > 0 else down)

    def o_forward(d, j, sign):
        to = (d + sign) % NZ
        oc[to, j] = send(o_full[d].at[j], o_full[to].at[j], up if sign > 0 else down)

    for j in range(2):
        z_forward(0, j, 1)
        z_forward(0, 1 - j, -1)
    for j in range(2):
        oc[0, j] = send(z_bufs[0].at[j], o_full[0].at[j], across)

    for copy in talk:
        copy.wait_recv()

    slot = [0]
    nu, nd = {}, {}

    def staged(src, pick):
        i = slot[0]
        slot[0] += 1
        stage[i] = src[pick]
        return stage.at[i]

    def x_forward(d):
        a = staged(z_bufs[d], choice(tabs.at[0], 0, -d))
        b = staged(z_bufs[d], choice(tabs.at[1], 0, -d))
        nd[d] = send(a, near_down.at[d], right)
        nu[d] = send(b, near_up.at[d], left)

    def z_arrive(d, j, sign=None):
        zc[d, j].wait_recv()
        if sign is not None:
            z_forward(d, j, sign)

    def o_arrive(d, j, sign=None):
        oc[d, j].wait_recv()
        if sign is not None:
            o_forward(d, j, sign)

    def rows_of(rel, d):
        if rel == 0:
            return lambda k: z_bufs[d][choice_of[0, d], :, k]
        if rel == 1:
            return lambda k: near_up[d, :, k]
        if rel == 3:
            return lambda k: near_down[d, :, k]
        if d in o_full:
            return lambda k: o_full[d][choice_of[2, d], :, k]
        return lambda k: o_sel[d - 3, :, k]

    choice_of = {}

    def settle(rel, d):
        choice_of[rel, d] = choice(table, rel, -d)

    starts = [sum(len(group) for group in GROUPS[:g]) for g in range(len(GROUPS))]

    def multiply_part(g, start, stop, first):
        k = pl.ds(start, stop - start)
        lhs = jnp.concatenate([rows_of(*tile)(k) for tile in GROUPS[g]], axis=0)
        got = lax.dot_general(lhs, train[:, k], (((1,), (1,)), ((), ())), preferred_element_type=jnp.float32)
        for i in range(len(GROUPS[g])):
            s, tile = starts[g] + i, got[i * 32 : (i + 1) * 32]
            scores[s] = tile if first else scores[s] + tile

    swaps, moves = {}, {}

    def swap(g):
        tiles = pl.ds(starts[g], len(GROUPS[g]))
        swaps[g] = send(scores.at[tiles, pl.ds(pl.multiple_of((1 - c) * HALF, HALF), HALF)], other.at[tiles], partner)

    def multiply(g):
        for start in range(0, width, CHUNK):
            multiply_part(g, start, min(start + CHUNK, width), start == 0)
        swap(g)

    mine = pl.ds(pl.multiple_of(c * HALF, HALF), HALF)

    def lanes_of(chip):
        return pl.ds(pl.multiple_of(chip * LANES, LANES), LANES)

    def spread(g):
        tiles = pl.ds(starts[g], len(GROUPS[g]))
        swaps[g].wait_recv()
        both[tiles] = scores[tiles, mine] + other[tiles]
        for dy in (2, 1, 3):
            src = both.at[tiles, :, lanes_of((y + dy) % NY)]
            moves[g, dy] = send(src, parts.at[dy - 1, tiles], ys[dy, 0])

    def finish(g):
        tiles = pl.ds(starts[g], len(GROUPS[g]))
        block = (tiles, mine, lanes_of(y))
        for dy in (1, 3, 2):
            moves[g, dy].wait_recv()
        total = both[tiles, :, lanes_of(y)]
        final[block] = total + parts[0, tiles] + parts[2, tiles] + parts[1, tiles]
        gathers[g] = [send(final.at[block], final.at[block], ys[dy, 0]) for dy in (2, 1, 3)]

    def relay(g):
        tiles = pl.ds(starts[g], len(GROUPS[g]))
        for copy in gathers[g]:
            copy.wait_recv()
        relays.append(send(final.at[tiles, mine], final.at[tiles, mine], partner))

    others = [(2, 0), (2, 1), (1, 0), (1, 1), (3, 0), (3, 1), (0, 1)]

    def spread_late(g):
        tiles = pl.ds(starts[g], len(GROUPS[g]))
        for i, (dy, dc) in enumerate(others):
            rows = pl.ds(pl.multiple_of((c + dc) % 2 * HALF, HALF), HALF)
            src = scores.at[tiles, rows, lanes_of((y + dy) % NY)]
            moves[g, i] = send(src, lates.at[i], ys[dy, dc])

    def finish_late(g):
        tiles = pl.ds(starts[g], len(GROUPS[g]))
        block = (tiles, mine, lanes_of(y))
        total = scores[block]
        for i in (6, 2, 3, 4, 5, 0, 1):
            moves[g, i].wait_recv()
            total = total + lates[i]
        final[block] = total
        for peer in others:
            relays.append(send(final.at[block], final.at[block], ys[peer]))

    def near(*levels):
        for d in levels:
            nu[d].wait_recv()
            nd[d].wait_recv()

    gathers, relays = {}, []
    x_forward(0)
    z_arrive(1, 0, 1)
    z_arrive(7, 1, -1)
    z_arrive(1, 1, 1)
    z_arrive(7, 0, -1)
    x_forward(1)
    x_forward(7)
    for d in (0, 1, 2, 6, 7):
        settle(2, d)
    for d in range(NZ):
        settle(0, d)
    z_arrive(2, 0, 1)
    z_arrive(6, 1, -1)
    z_arrive(2, 1, 1)
    z_arrive(6, 0, -1)
    x_forward(2)
    x_forward(6)
    o_arrive(0, 0)
    o_arrive(0, 1)
    train_copy.wait()
    near(0)
    multiply(0)
    z_arrive(3, 0, 1)
    z_arrive(5, 1, -1)
    for j in range(2):
        o_forward(0, j, 1)
        o_forward(0, j, -1)
    spread(0)
    z_arrive(3, 1)
    z_arrive(5, 0)
    x_forward(3)
    x_forward(5)
    near(1, 7)
    multiply(1)
    finish(0)
    z_arrive(4, 0)
    z_arrive(4, 1)
    x_forward(4)
    oc[4] = send(staged(z_bufs[4], choice(tabs.at[2], 0, -4)), o_sel.at[1], across)

    def o_part(src, d, part, peer):
        k = pl.ds(SPLIT[part], SPLIT[part + 1] - SPLIT[part])
        return send(src.at[:, k], o_sel.at[d - 3, :, k], peer)

    for d in (3, 5):
        oc[d] = [o_part(staged(z_bufs[d], choice(tabs.at[2], 0, -d)), d, 2, across)]
    spread(1)
    near(2, 6)
    multiply(2)
    relay(0)
    o_arrive(1, 0, 1)
    o_arrive(7, 0, -1)
    spread(2)
    finish(1)
    o_arrive(1, 1, 1)
    o_arrive(7, 1, -1)
    multiply(4)
    finish(2)
    near(3, 5)
    multiply(3)
    relay(1)
    spread(4)
    spread(3)
    near(4)
    multiply(5)
    finish(4)
    relay(2)
    spread(5)
    for d in (2, 6):
        for j in range(2):
            o_arrive(d, j)
    a = staged(o_full[2], choice(tabs.at[3], 2, -2))
    b = staged(o_full[6], choice(tabs.at[4], 2, 2))
    for part in range(2):
        oc[3].append(o_part(a, 3, part, up))
        oc[5].append(o_part(b, 5, part, down))
    finish(3)
    oc[4].wait_recv()
    multiply(6)
    finish(5)
    relay(4)
    relay(3)
    spread(6)
    for i, part in enumerate((0, 2, 1)):
        for d in (3, 5):
            oc[d][(1, 0, 2)[i]].wait_recv()
        multiply_part(7, SPLIT[part], SPLIT[part + 1], i == 0)
    spread_late(7)
    finish(6)
    relay(5)
    finish_late(7)
    relay(6)
    done = len(sent) - 16
    for copy in sent[:done]:
        copy.wait_send()
    for copy in relays:
        copy.wait_recv()
    for i in range(4):
        k = 4 * feat + i
        holder = lax.rem(stored_of(k), HOLDERS)
        rel = lax.rem(lax.div(holder, NZ) - x + NX, NX)
        d = lax.rem(z - lax.rem(holder, NZ) + NZ, NZ)
        out[0, i] = jnp.where(k < counts[0], final[place[rel * NZ + d]], 0.0)
    for copy in sent[done:]:
        copy.wait_send()


def shards(train_grads, audit_grads, owner_map, pair_blocks, pair_counts):
    rows, width = train_grads.shape
    block = (audit_grads.shape[2], width)
    half = pltpu.VMEM
    scratch = [
        half((rows, width), jnp.bfloat16),
        half((8, 128), jnp.int32),
        half((5, 8, 128), jnp.int32),
        half((HOLDERS, block[0], rows), jnp.float32),
        half((HOLDERS, HALF, rows), jnp.float32),
        half((HOLDERS, HALF, rows), jnp.float32),
        half((NY - 1, HOLDERS, HALF, LANES), jnp.float32),
        half((7, 2, HALF, LANES), jnp.float32),
        half((HOLDERS, block[0], rows), jnp.float32),
        pltpu.SMEM((HOLDERS,), jnp.int32),
        pltpu.SemaphoreType.DMA((MESSAGES,)),
        pltpu.SemaphoreType.DMA((MESSAGES,)),
        pltpu.SemaphoreType.DMA((2,)),
    ]
    scratch += [half((2,) + block, jnp.bfloat16) for _ in range(NZ + 5)]
    scratch += [
        half((3,) + block, jnp.bfloat16),
        half((NZ,) + block, jnp.bfloat16),
        half((NZ,) + block, jnp.bfloat16),
        half((21,) + block, jnp.bfloat16),
    ]
    return pl.pallas_call(
        kernel,
        out_shape=jax.ShapeDtypeStruct((1, 4, block[0], rows), jnp.float32),
        in_specs=[pl.BlockSpec(memory_space=pl.ANY)] * 2 + [pl.BlockSpec(memory_space=pltpu.SMEM)] * 3,
        out_specs=pl.BlockSpec(memory_space=pltpu.VMEM),
        scratch_shapes=scratch,
        compiler_params=pltpu.CompilerParams(collective_id=0, has_side_effects=True, vmem_limit_bytes=60000 * 1024),
    )(train_grads, audit_grads, owner_map, pair_blocks, pair_counts)


def solution(mesh):
    in_specs = (P("ex", "feat"), P(None, "ex", None, "feat"), P(), P("ex", None), P("ex"))
    out_specs = P("ex", "feat", None, None)
    return jax.shard_map(shards, mesh=mesh, in_specs=in_specs, out_specs=out_specs, check_vma=False)
```

```python
import functools

import jax
import jax.numpy as jnp
from jax import lax
from jax.experimental import pallas as pl
from jax.experimental.pallas import tpu as pltpu
from jax.sharding import PartitionSpec as P

MESH = pl.DeviceIdType.MESH
NX, NZ, NY = 4, 8, 4
HOLDERS = NX * NZ
MESSAGES = 58
HALF, LANES = 16, 128
GROUPS = (
    ((0, 0), (1, 0), (3, 0), (2, 0)),
    ((0, 1), (1, 1), (3, 1), (0, 7), (1, 7), (3, 7)),
    ((0, 2), (1, 2), (3, 2), (0, 6), (1, 6), (3, 6)),
    ((0, 3), (1, 3), (3, 3), (0, 5), (1, 5), (3, 5)),
    ((2, 1), (2, 7)),
    ((0, 4), (1, 4), (3, 4)),
    ((2, 2), (2, 6), (2, 4)),
    ((2, 3), (2, 5)),
)
ORDER = [tile for group in GROUPS for tile in group]
SPLIT = (0, 2048, 2688, 4096)
CHUNK = 1024


def kernel(train_hbm, audit_hbm, owner, pairs, counts, out, *scratch):
    (train, table, tabs, scores, other, both, parts, lates, final, place, send_sem, recv_sem, local_sem) = scratch[:13]
    z_bufs = scratch[13:21]
    o_full = dict(zip((0, 1, 2, 6, 7), scratch[21:26]))
    o_sel, near_up, near_down, stage = scratch[26:30]
    ex, feat = lax.axis_index("ex"), lax.axis_index("feat")
    x, z, y, c = ex // NZ, ex % NZ, feat // 2, feat % 2
    width = train.shape[1]

    def at(dx=0, dz=0, dy=0, dc=0):
        px, pz = (x + dx + NX) % NX, (z + dz + NZ) % NZ
        py, pc = (y + dy + NY) % NY, (c + dc) % 2
        return (px * NZ + pz, py * 2 + pc)

    right, left, across = at(dx=1), at(dx=-1), at(dx=2)
    up, down, partner = at(dz=1), at(dz=-1), at(dc=1)
    ys = {(dy, dc): at(dy=dy, dc=dc) for dy in (1, 2, 3) for dc in (0, 1)}
    ys[0, 1] = partner

    barrier = pltpu.get_barrier_semaphore()
    everyone = [right, left, across, up, down] + list(ys.values())
    for peer in everyone:
        pl.semaphore_signal(barrier, inc=1, device_id=peer, device_id_type=MESH)
    own_copy = pltpu.make_async_copy(audit_hbm.at[:, 0], z_bufs[0], local_sem.at[0])
    own_copy.start()
    train_copy = pltpu.make_async_copy(train_hbm, train, local_sem.at[1])
    train_copy.start()

    def stored_of(k):
        return owner[pairs[0, k]]

    lane = lax.broadcasted_iota(jnp.int32, (8, 128), 1)
    picks = jnp.zeros((8, 128), jnp.int32)
    for k in range(HOLDERS):
        stored = stored_of(k)
        picks = jnp.where(lane == lax.rem(stored, HOLDERS), lax.div(stored, HOLDERS), picks)
    table[...] = picks
    for i, (rel, d) in enumerate(ORDER):
        place[rel * NZ + d] = i

    def choice(ref, dx, dz):
        holder = (x + dx + NX) % NX * NZ + (z + dz + NZ) % NZ
        return jnp.max(jnp.where(lane == holder, ref[...], 0))

    flights = {}

    def copy_of(key, src, dst, peer):
        i = flights[key][0]
        return pltpu.make_async_remote_copy(
            src_ref=src, dst_ref=dst, send_sem=send_sem.at[i], recv_sem=recv_sem.at[i], device_id=peer, device_id_type=MESH
        )

    def send(key, src, dst, peer, whole=None):
        if key not in flights:
            flights[key] = len(flights), dst if whole is None else whole
        copy_of(key, src, dst, peer).start()

    def flight(key):
        return copy_of(key, flights[key][1], flights[key][1], partner)

    def arrive(key):
        flight(key).wait_recv()

    pl.semaphore_wait(barrier, len(everyone))
    own_copy.wait()

    for seat, peer in ((1, right), (0, left), (2, across), (4, up), (3, down)):
        send("talk", table, tabs.at[seat], peer, tabs)

    def z_forward(d, j, sign):
        to = (d + sign) % NZ
        send(("z", to, j), z_bufs[d].at[j], z_bufs[to].at[j], up if sign > 0 else down)

    def o_forward(d, j, sign):
        to, k = (d + sign) % NZ, pl.ds(j * width // 2, width // 2)
        send(("o", to, j), o_full[d].at[:, :, k], o_full[to].at[:, :, k], up if sign > 0 else down)

    for j in range(2):
        z_forward(0, j, 1)
        z_forward(0, 1 - j, -1)
    for j in range(2):
        send("o", z_bufs[0].at[j], o_full[0].at[j], across, o_full[0])
    arrive("talk")

    slot = [0]

    def staged(src, pick, k=slice(None), part=False):
        i = slot[0]
        slot[0] += 1
        stage[i, :, k] = jnp.where(pick > 0, src[1, :, k], src[0, :, k]) if part else src[pick, :, k]
        return stage.at[i]

    def x_forward(d):
        a = staged(z_bufs[d], choice(tabs.at[0], 0, -d))
        b = staged(z_bufs[d], choice(tabs.at[1], 0, -d))
        level = min(d, NZ - d)
        whole = near_up.at[pl.ds(0, 2 if level in (0, 4) else 4)]
        send(("n", level), a, near_down.at[d], right, whole)
        send(("n", level), b, near_up.at[d], left, whole)

    def z_arrive(d, j, sign=None):
        arrive(("z", d, j))
        if sign is not None:
            z_forward(d, j, sign)

    def o_arrive(d, j, sign=None):
        arrive(("o", d, j))
        if sign is not None:
            o_forward(d, j, sign)

    def rows_of(rel, d):
        if rel == 0:
            return lambda k: z_bufs[d][choice_of[0, d], :, k]
        if rel == 1:
            return lambda k: near_up[d, :, k]
        if rel == 3:
            return lambda k: near_down[d, :, k]
        if d in o_full:
            return lambda k: o_full[d][choice_of[2, d], :, k]
        return lambda k: o_sel[d - 3, :, k]

    choice_of = {}

    def settle(rel, d):
        choice_of[rel, d] = choice(table, rel, -d)

    starts = [sum(len(group) for group in GROUPS[:g]) for g in range(len(GROUPS))]

    def multiply_part(g, start, stop, first):
        k = pl.ds(start, stop - start)
        lhs = jnp.concatenate([rows_of(*tile)(k) for tile in GROUPS[g]], axis=0)
        got = lax.dot_general(lhs, train[:, k], (((1,), (1,)), ((), ())), preferred_element_type=jnp.float32)
        for i in range(len(GROUPS[g])):
            s, tile = starts[g] + i, got[i * 32 : (i + 1) * 32]
            scores[s] = tile if first else scores[s] + tile

    def swap(g):
        tiles = pl.ds(starts[g], len(GROUPS[g]))
        send(("swap", g), scores.at[tiles, pl.ds(pl.multiple_of((1 - c) * HALF, HALF), HALF)], other.at[tiles], partner)

    def multiply(g):
        for start in range(0, width, CHUNK):
            multiply_part(g, start, min(start + CHUNK, width), start == 0)
        swap(g)

    mine = pl.ds(pl.multiple_of(c * HALF, HALF), HALF)

    def lanes_of(chip):
        return pl.ds(pl.multiple_of(chip * LANES, LANES), LANES)

    def spread(g):
        tiles = pl.ds(starts[g], len(GROUPS[g]))
        arrive(("swap", g))
        both[tiles] = scores[tiles, mine] + other[tiles]
        for dy in (2, 1, 3):
            src = both.at[tiles, :, lanes_of((y + dy) % NY)]
            send(("spread", g), src, parts.at[dy - 1, tiles], ys[dy, 0], parts.at[:, tiles])

    def finish(g):
        tiles = pl.ds(starts[g], len(GROUPS[g]))
        block = (tiles, mine, lanes_of(y))
        arrive(("spread", g))
        total = both[tiles, :, lanes_of(y)]
        final[block] = total + parts[0, tiles] + parts[2, tiles] + parts[1, tiles]
        for dy in (2, 1, 3):
            send(("gather", g), final.at[block], final.at[block], ys[dy, 0], parts.at[:, tiles])

    def relay(g):
        tiles = pl.ds(starts[g], len(GROUPS[g]))
        arrive(("gather", g))
        send("relay", final.at[tiles, mine], final.at[tiles, mine], partner, other.at[pl.ds(0, starts[-1])])

    others = [(2, 0), (2, 1), (1, 0), (1, 1), (3, 0), (3, 1), (0, 1)]

    def spread_late(g):
        tiles = pl.ds(starts[g], len(GROUPS[g]))
        for i, (dy, dc) in enumerate(others):
            rows = pl.ds(pl.multiple_of((c + dc) % 2 * HALF, HALF), HALF)
            src = scores.at[tiles, rows, lanes_of((y + dy) % NY)]
            send("late", src, lates.at[i], ys[dy, dc], lates)

    def finish_late(g):
        tiles = pl.ds(starts[g], len(GROUPS[g]))
        block = (tiles, mine, lanes_of(y))
        total = scores[block]
        arrive("late")
        for i in range(7):
            total = total + lates[i]
        final[block] = total
        for peer in others:
            send("end", final.at[block], final.at[block], ys[peer], lates)

    x_forward(0)
    z_arrive(1, 0, 1)
    z_arrive(7, 1, -1)
    z_arrive(1, 1, 1)
    z_arrive(7, 0, -1)
    x_forward(1)
    x_forward(7)
    for d in (0, 1, 2, 6, 7):
        settle(2, d)
    for d in range(NZ):
        settle(0, d)
    z_arrive(2, 0, 1)
    z_arrive(6, 1, -1)
    z_arrive(2, 1, 1)
    z_arrive(6, 0, -1)
    x_forward(2)
    x_forward(6)
    arrive("o")
    train_copy.wait()
    arrive(("n", 0))
    multiply(0)
    z_arrive(3, 0, 1)
    z_arrive(5, 1, -1)
    for j in range(2):
        o_forward(0, j, 1)
        o_forward(0, j, -1)
    spread(0)
    z_arrive(3, 1)
    z_arrive(5, 0)
    x_forward(3)
    x_forward(5)
    arrive(("n", 1))
    multiply(1)
    finish(0)
    z_arrive(4, 0)
    z_arrive(4, 1)
    x_forward(4)
    send("o4", staged(z_bufs[4], choice(tabs.at[2], 0, -4)), o_sel.at[1], across)

    def o_part(src, d, part, peer):
        k = pl.ds(SPLIT[part], SPLIT[part + 1] - SPLIT[part])
        send(("o3", part), src.at[:, k], o_sel.at[d - 3, :, k], peer, near_up.at[pl.ds(0, 2), :, k])

    for d in (3, 5):
        o_part(staged(z_bufs[d], choice(tabs.at[2], 0, -d), slice(SPLIT[2], width)), d, 2, across)
    spread(1)
    arrive(("n", 2))
    multiply(2)
    relay(0)
    o_arrive(1, 0, 1)
    o_arrive(7, 0, -1)
    spread(2)
    finish(1)
    o_arrive(1, 1, 1)
    o_arrive(7, 1, -1)
    multiply(4)
    finish(2)
    arrive(("n", 3))
    multiply(3)
    relay(1)
    spread(4)
    above, below = choice(tabs.at[3], 2, -2), choice(tabs.at[4], 2, 2)

    def far_last(part):
        k = slice(SPLIT[part], SPLIT[part + 1])
        o_arrive(2, part)
        o_part(staged(o_full[2], above, k, True), 3, part, up)
        o_arrive(6, part)
        o_part(staged(o_full[6], below, k, True), 5, part, down)

    far_last(0)
    spread(3)
    arrive(("n", 4))
    multiply(5)
    finish(4)
    relay(2)
    spread(5)
    far_last(1)
    finish(3)
    arrive("o4")
    multiply(6)
    finish(5)
    spread(6)
    for i, part in enumerate((0, 2, 1)):
        arrive(("o3", part))
        multiply_part(7, SPLIT[part], SPLIT[part + 1], i == 0)
    spread_late(7)
    finish(6)
    relay(4)
    relay(3)
    relay(5)
    finish_late(7)
    relay(6)
    old = [key for key in flights if key not in ("relay", "end")]
    for key in old:
        flight(key).wait_send()
    arrive("relay")
    arrive("end")
    for i in range(4):
        k = 4 * feat + i
        holder = lax.rem(stored_of(k), HOLDERS)
        rel = lax.rem(lax.div(holder, NZ) - x + NX, NX)
        d = lax.rem(z - lax.rem(holder, NZ) + NZ, NZ)
        out[0, i] = jnp.where(k < counts[0], final[place[rel * NZ + d]], 0.0)
    flight("relay").wait_send()
    flight("end").wait_send()


def shards(train_grads, audit_grads, owner_map, pair_blocks, pair_counts):
    rows, width = train_grads.shape
    block = (audit_grads.shape[2], width)
    half = pltpu.VMEM
    scratch = [
        half((rows, width), jnp.bfloat16),
        half((8, 128), jnp.int32),
        half((5, 8, 128), jnp.int32),
        half((HOLDERS, block[0], rows), jnp.float32),
        half((HOLDERS, HALF, rows), jnp.float32),
        half((HOLDERS, HALF, rows), jnp.float32),
        half((NY - 1, HOLDERS, HALF, LANES), jnp.float32),
        half((7, 2, HALF, LANES), jnp.float32),
        half((HOLDERS, block[0], rows), jnp.float32),
        pltpu.SMEM((HOLDERS,), jnp.int32),
        pltpu.SemaphoreType.DMA((MESSAGES,)),
        pltpu.SemaphoreType.DMA((MESSAGES,)),
        pltpu.SemaphoreType.DMA((2,)),
    ]
    scratch += [half((2,) + block, jnp.bfloat16) for _ in range(NZ + 5)]
    scratch += [
        half((3,) + block, jnp.bfloat16),
        half((NZ,) + block, jnp.bfloat16),
        half((NZ,) + block, jnp.bfloat16),
        half((23,) + block, jnp.bfloat16),
    ]
    return pl.pallas_call(
        kernel,
        out_shape=jax.ShapeDtypeStruct((1, 4, block[0], rows), jnp.float32),
        in_specs=[pl.BlockSpec(memory_space=pl.ANY)] * 2 + [pl.BlockSpec(memory_space=pltpu.SMEM)] * 3,
        out_specs=pl.BlockSpec(memory_space=pltpu.VMEM),
        scratch_shapes=scratch,
        compiler_params=pltpu.CompilerParams(collective_id=0, has_side_effects=True, vmem_limit_bytes=60000 * 1024),
    )(train_grads, audit_grads, owner_map, pair_blocks, pair_counts)


def solution(mesh):
    in_specs = (P("ex", "feat"), P(None, "ex", None, "feat"), P(), P("ex", None), P("ex"))
    out_specs = P("ex", "feat", None, None)
    return jax.shard_map(shards, mesh=mesh, in_specs=in_specs, out_specs=out_specs, check_vma=False)
```

```python
import functools

import jax
import jax.numpy as jnp
from jax import lax
from jax.experimental import pallas as pl
from jax.experimental.pallas import tpu as pltpu
from jax.sharding import PartitionSpec as P

MESH = pl.DeviceIdType.MESH
NX, NZ, NY = 4, 8, 4
HOLDERS = NX * NZ
MESSAGES = 57
HALF, LANES = 16, 128
GROUPS = (
    ((0, 0), (1, 0), (3, 0), (2, 0)),
    ((0, 1), (1, 1), (3, 1), (0, 7), (1, 7), (3, 7)),
    ((0, 2), (1, 2), (3, 2), (0, 6), (1, 6), (3, 6)),
    ((0, 3), (1, 3), (3, 3), (0, 5), (1, 5), (3, 5)),
    ((2, 1), (2, 7)),
    ((0, 4), (1, 4), (3, 4)),
    ((2, 2), (2, 6), (2, 4)),
    ((2, 3), (2, 5)),
)
ORDER = [tile for group in GROUPS for tile in group]
SPLIT = (0, 2048, 2560, 4096)
CHUNK = 1024


def kernel(train_hbm, audit_hbm, owner_hbm, pairs_hbm, counts_hbm, out, *scratch):
    owner, pairs, counts = scratch[30:33]
    (train, table, tabs, scores, other, both, parts, lates, final, place, send_sem, recv_sem, local_sem) = scratch[:13]
    z_bufs = scratch[13:21]
    o_full = dict(zip((0, 1, 2, 6, 7), scratch[21:26]))
    o_sel, near_up, near_down, stage = scratch[26:30]
    ex, feat = lax.axis_index("ex"), lax.axis_index("feat")
    x, z, y, c = ex // NZ, ex % NZ, feat // 2, feat % 2
    width = train.shape[1]

    def at(dx=0, dz=0, dy=0, dc=0):
        px, pz = (x + dx + NX) % NX, (z + dz + NZ) % NZ
        py, pc = (y + dy + NY) % NY, (c + dc) % 2
        return (px * NZ + pz, py * 2 + pc)

    right, left, across = at(dx=1), at(dx=-1), at(dx=2)
    up, down, partner = at(dz=1), at(dz=-1), at(dc=1)
    ys = {(dy, dc): at(dy=dy, dc=dc) for dy in (1, 2, 3) for dc in (0, 1)}
    ys[0, 1] = partner

    barrier = pltpu.get_barrier_semaphore()
    everyone = [right, left, across, up, down] + list(ys.values())
    for peer in everyone:
        pl.semaphore_signal(barrier, inc=1, device_id=peer, device_id_type=MESH)
    own_copy = pltpu.make_async_copy(audit_hbm.at[:, 0], z_bufs[0], local_sem.at[0])
    own_copy.start()
    lists = ((owner_hbm, owner), (pairs_hbm, pairs), (counts_hbm, counts))
    list_copies = [pltpu.make_async_copy(src, dst, local_sem.at[2 + i]) for i, (src, dst) in enumerate(lists)]
    for copy in list_copies:
        copy.start()
    train_copy = pltpu.make_async_copy(train_hbm, train, local_sem.at[1])
    train_copy.start()

    for copy in list_copies:
        copy.wait()

    def stored_of(k):
        return owner[pairs[0, k]]

    lane = lax.broadcasted_iota(jnp.int32, (8, 128), 1)
    picks = jnp.zeros((8, 128), jnp.int32)
    for k in range(HOLDERS):
        stored = stored_of(k)
        picks = jnp.where(lane == lax.rem(stored, HOLDERS), lax.div(stored, HOLDERS), picks)
    table[...] = picks
    for i, (rel, d) in enumerate(ORDER):
        place[rel * NZ + d] = i

    def choice(ref, dx, dz):
        holder = (x + dx + NX) % NX * NZ + (z + dz + NZ) % NZ
        return jnp.max(jnp.where(lane == holder, ref[...], 0))

    flights = {}

    def copy_of(key, src, dst, peer):
        i = flights[key][0]
        return pltpu.make_async_remote_copy(
            src_ref=src, dst_ref=dst, send_sem=send_sem.at[i], recv_sem=recv_sem.at[i], device_id=peer, device_id_type=MESH
        )

    def send(key, src, dst, peer, whole=None):
        if key not in flights:
            flights[key] = len(flights), dst if whole is None else whole
        copy_of(key, src, dst, peer).start()

    def flight(key):
        return copy_of(key, flights[key][1], flights[key][1], partner)

    def arrive(key):
        flight(key).wait_recv()

    pl.semaphore_wait(barrier, len(everyone))
    own_copy.wait()

    for seat, peer in ((1, right), (0, left), (2, across), (4, up), (3, down)):
        send("talk", table, tabs.at[seat], peer, tabs)

    def z_forward(d, j, sign):
        to = (d + sign) % NZ
        send(("z", to, j), z_bufs[d].at[j], z_bufs[to].at[j], up if sign > 0 else down)

    def o_forward(d, j, sign):
        to, k = (d + sign) % NZ, pl.ds(j * width // 2, width // 2)
        send(("o", to, j), o_full[d].at[:, :, k], o_full[to].at[:, :, k], up if sign > 0 else down)

    for j in range(2):
        z_forward(0, j, 1)
        z_forward(0, 1 - j, -1)
    for j in range(2):
        send("o", z_bufs[0].at[j], o_full[0].at[j], across, o_full[0])
    arrive("talk")

    slot = [0]

    def staged(src, pick, k=slice(None), part=False):
        i = slot[0]
        slot[0] += 1
        stage[i, :, k] = jnp.where(pick > 0, src[1, :, k], src[0, :, k]) if part else src[pick, :, k]
        return stage.at[i]

    def x_forward(d):
        a = staged(z_bufs[d], choice(tabs.at[0], 0, -d))
        b = staged(z_bufs[d], choice(tabs.at[1], 0, -d))
        level = min(d, NZ - d)
        whole = near_up.at[pl.ds(0, 2 if level in (0, 4) else 4)]
        send(("n", level), a, near_down.at[d], right, whole)
        send(("n", level), b, near_up.at[d], left, whole)

    def z_arrive(d, j, sign=None):
        arrive(("z", d, j))
        if sign is not None:
            z_forward(d, j, sign)

    def o_arrive(d, j, sign=None):
        arrive(("o", d, j))
        if sign is not None:
            o_forward(d, j, sign)

    def rows_of(rel, d):
        if rel == 0:
            return lambda k: z_bufs[d][choice_of[0, d], :, k]
        if rel == 1:
            return lambda k: near_up[d, :, k]
        if rel == 3:
            return lambda k: near_down[d, :, k]
        if d in o_full:
            return lambda k: o_full[d][choice_of[2, d], :, k]
        return lambda k: o_sel[d - 3, :, k]

    choice_of = {}

    def settle(rel, d):
        choice_of[rel, d] = choice(table, rel, -d)

    starts = [sum(len(group) for group in GROUPS[:g]) for g in range(len(GROUPS))]

    def multiply_part(g, start, stop, first):
        k = pl.ds(start, stop - start)
        lhs = jnp.concatenate([rows_of(*tile)(k) for tile in GROUPS[g]], axis=0)
        got = lax.dot_general(lhs, train[:, k], (((1,), (1,)), ((), ())), preferred_element_type=jnp.float32)
        for i in range(len(GROUPS[g])):
            s, tile = starts[g] + i, got[i * 32 : (i + 1) * 32]
            scores[s] = tile if first else scores[s] + tile

    def swap(g):
        tiles = pl.ds(starts[g], len(GROUPS[g]))
        send(("swap", g), scores.at[tiles, pl.ds(pl.multiple_of((1 - c) * HALF, HALF), HALF)], other.at[tiles], partner)

    def multiply(g):
        for start in range(0, width, CHUNK):
            multiply_part(g, start, min(start + CHUNK, width), start == 0)
        swap(g)

    mine = pl.ds(pl.multiple_of(c * HALF, HALF), HALF)

    def lanes_of(chip):
        return pl.ds(pl.multiple_of(chip * LANES, LANES), LANES)

    def spread(g):
        tiles = pl.ds(starts[g], len(GROUPS[g]))
        arrive(("swap", g))
        both[tiles] = scores[tiles, mine] + other[tiles]
        for dy in (2, 1, 3):
            src = both.at[tiles, :, lanes_of((y + dy) % NY)]
            send(("spread", g), src, parts.at[dy - 1, tiles], ys[dy, 0], parts.at[:, tiles])

    def finish(g):
        tiles = pl.ds(starts[g], len(GROUPS[g]))
        block = (tiles, mine, lanes_of(y))
        arrive(("spread", g))
        total = both[tiles, :, lanes_of(y)]
        final[block] = total + parts[0, tiles] + parts[2, tiles] + parts[1, tiles]
        for dy in (2, 1, 3):
            send(("gather", g), final.at[block], final.at[block], ys[dy, 0], parts.at[:, tiles])

    def relay(g):
        tiles = pl.ds(starts[g], len(GROUPS[g]))
        arrive(("gather", g))
        send("relay", final.at[tiles, mine], final.at[tiles, mine], partner, other.at[pl.ds(0, starts[-1])])

    others = [(2, 0), (2, 1), (1, 0), (1, 1), (3, 0), (3, 1), (0, 1)]

    def spread_late(g):
        tiles = pl.ds(starts[g], len(GROUPS[g]))
        for i, (dy, dc) in enumerate(others):
            rows = pl.ds(pl.multiple_of((c + dc) % 2 * HALF, HALF), HALF)
            src = scores.at[tiles, rows, lanes_of((y + dy) % NY)]
            send("late", src, lates.at[i], ys[dy, dc], lates)

    def finish_late(g):
        tiles = pl.ds(starts[g], len(GROUPS[g]))
        block = (tiles, mine, lanes_of(y))
        total = scores[block]
        arrive("late")
        for i in range(7):
            total = total + lates[i]
        final[block] = total
        for peer in others:
            send("end", final.at[block], final.at[block], ys[peer], lates)

    x_forward(0)
    z_arrive(1, 0, 1)
    z_arrive(7, 1, -1)
    z_arrive(1, 1, 1)
    z_arrive(7, 0, -1)
    x_forward(1)
    x_forward(7)
    for d in (0, 1, 2, 6, 7):
        settle(2, d)
    for d in range(NZ):
        settle(0, d)
    z_arrive(2, 0, 1)
    z_arrive(6, 1, -1)
    z_arrive(2, 1, 1)
    z_arrive(6, 0, -1)
    x_forward(2)
    x_forward(6)
    arrive("o")
    train_copy.wait()
    arrive(("n", 0))
    multiply(0)
    z_arrive(3, 0, 1)
    z_arrive(5, 1, -1)
    for j in range(2):
        o_forward(0, j, 1)
        o_forward(0, j, -1)
    spread(0)
    z_arrive(3, 1)
    z_arrive(5, 0)
    x_forward(3)
    x_forward(5)
    arrive(("n", 1))
    multiply(1)
    finish(0)
    z_arrive(4, 0)
    z_arrive(4, 1)
    x_forward(4)
    send("o4", staged(z_bufs[4], choice(tabs.at[2], 0, -4)), o_sel.at[1], across)

    def o_part(src, d, part, peer):
        k = pl.ds(SPLIT[part], SPLIT[part + 1] - SPLIT[part])
        send(("o3", part), src.at[:, k], o_sel.at[d - 3, :, k], peer, near_up.at[pl.ds(0, 2), :, k])

    for d in (3, 5):
        o_part(staged(z_bufs[d], choice(tabs.at[2], 0, -d), slice(SPLIT[2], width)), d, 2, across)
    spread(1)
    arrive(("n", 2))
    multiply(2)
    relay(0)
    o_arrive(1, 0, 1)
    o_arrive(7, 0, -1)
    spread(2)
    finish(1)
    o_arrive(1, 1, 1)
    o_arrive(7, 1, -1)
    multiply(4)
    finish(2)
    arrive(("n", 3))
    multiply(3)
    relay(1)
    spread(4)
    above, below = choice(tabs.at[3], 2, -2), choice(tabs.at[4], 2, 2)

    def far_last(part):
        k = slice(SPLIT[part], SPLIT[part + 1])
        o_arrive(2, part)
        o_part(staged(o_full[2], above, k, True), 3, part, up)
        o_arrive(6, part)
        o_part(staged(o_full[6], below, k, True), 5, part, down)

    far_last(0)
    spread(3)
    arrive(("n", 4))
    multiply(5)
    finish(4)
    relay(2)
    spread(5)
    far_last(1)
    finish(3)
    arrive("o4")
    multiply(6)
    finish(5)
    spread(6)
    for i, part in enumerate((0, 2, 1)):
        arrive(("o3", part))
        multiply_part(7, SPLIT[part], SPLIT[part + 1], i == 0)
    spread_late(7)
    finish(6)
    relay(4)
    relay(3)
    relay(5)
    finish_late(7)
    relay(6)
    old = [key for key in flights if key not in ("relay", "end")]
    for key in old:
        flight(key).wait_send()
    arrive("relay")
    arrive("end")
    for i in range(4):
        k = 4 * feat + i
        holder = lax.rem(stored_of(k), HOLDERS)
        rel = lax.rem(lax.div(holder, NZ) - x + NX, NX)
        d = lax.rem(z - lax.rem(holder, NZ) + NZ, NZ)
        out[0, i] = jnp.where(k < counts[0], final[place[rel * NZ + d]], 0.0)
    flight("relay").wait_send()
    flight("end").wait_send()


def shards(train_grads, audit_grads, owner_map, pair_blocks, pair_counts):
    rows, width = train_grads.shape
    block = (audit_grads.shape[2], width)
    half = pltpu.VMEM
    scratch = [
        half((rows, width), jnp.bfloat16),
        half((8, 128), jnp.int32),
        half((5, 8, 128), jnp.int32),
        half((HOLDERS, block[0], rows), jnp.float32),
        half((HOLDERS, HALF, rows), jnp.float32),
        half((HOLDERS, HALF, rows), jnp.float32),
        half((NY - 1, HOLDERS, HALF, LANES), jnp.float32),
        half((7, 2, HALF, LANES), jnp.float32),
        half((HOLDERS, block[0], rows), jnp.float32),
        pltpu.SMEM((HOLDERS,), jnp.int32),
        pltpu.SemaphoreType.DMA((MESSAGES,)),
        pltpu.SemaphoreType.DMA((MESSAGES,)),
        pltpu.SemaphoreType.DMA((5,)),
    ]
    scratch += [half((2,) + block, jnp.bfloat16) for _ in range(NZ + 5)]
    scratch += [
        half((3,) + block, jnp.bfloat16),
        half((NZ,) + block, jnp.bfloat16),
        half((NZ,) + block, jnp.bfloat16),
        half((23,) + block, jnp.bfloat16),
    ]
    scratch += [pltpu.SMEM(a.shape, jnp.int32) for a in (owner_map, pair_blocks, pair_counts)]
    return pl.pallas_call(
        kernel,
        out_shape=jax.ShapeDtypeStruct((1, 4, block[0], rows), jnp.float32),
        in_specs=[pl.BlockSpec(memory_space=pl.ANY)] * 5,
        out_specs=pl.BlockSpec(memory_space=pltpu.VMEM),
        scratch_shapes=scratch,
        compiler_params=pltpu.CompilerParams(collective_id=0, has_side_effects=True, vmem_limit_bytes=60000 * 1024),
    )(train_grads, audit_grads, owner_map, pair_blocks, pair_counts)


def solution(mesh):
    in_specs = (P("ex", "feat"), P(None, "ex", None, "feat"), P(), P("ex", None), P("ex"))
    out_specs = P("ex", "feat", None, None)
    return jax.shard_map(shards, mesh=mesh, in_specs=in_specs, out_specs=out_specs, check_vma=False)
```
